256 devices in a mesh: view: 32 (over y, x, core), strip: 8 (over z).
Axes of the slice: x: 4, y: 4, z: 8, core: 2. Of those that a mesh axis runs over, the one named last changes fastest.
Arguments:
- tokens: bfloat16 [32, 1024, 1536], P('view', 'strip'), may hold values from -48 to 48
- source_ids: int32 [32, 8, 5], replicated, may hold values from 0 to 255, as said below
- source_count: int32 [32, 8], replicated, may hold values from 2 to 5, as said below
- self_query: bfloat16 [1536, 1536], P(None, 'strip'), may hold values from -24 to 24
- self_key: bfloat16 [1536, 1536], P(None, 'strip'), may hold values from -24 to 24
- self_value: bfloat16 [1536, 1536], P(None, 'strip'), may hold values from -0.15625 to 0.15625
- self_out: bfloat16 [1536, 1536], P('strip'), may hold values from -1.1953125 to 1.1953125
- cross_query: bfloat16 [1536, 1536], P(None, 'strip'), may hold values from -24 to 24
- cross_key: bfloat16 [1536, 1536], P(None, 'strip'), may hold values from -24 to 24
- cross_value: bfloat16 [1536, 1536], P(None, 'strip'), may hold values from -0.15625 to 0.15625
- cross_out: bfloat16 [1536, 1536], P('strip'), may hold values from -1.1953125 to 1.1953125
- mlp_up: bfloat16 [1536, 6144], P(None, 'strip'), may hold values from -0.15625 to 0.15625
- mlp_down: bfloat16 [6144, 1536], P('strip'), may hold values from -0.078125 to 0.078125
Outputs:
- mixed: bfloat16 [32, 1024, 1536], P('view', 'strip')
The draws below stay inside these ranges and needn't reach their ends.
Inputs may be any that keep to these rules, and one draw needn't show every extreme that they name: `source_ids`: entry k of strip s of view v names a strip of another view than v; entries with k >= source_count[v, s] are unused. Among all 40 entries of one destination view, used or not, each other view is named at most 2 times, and some view exactly 2 times. `source_count`: every view has a strip with all 5 entries in use.
All inputs are finite; a program needn't handle non-finite values.
Results may differ from the reference program's by a relative error of at most 0.015.
Values may be sent and summed in bfloat16 or wider, within the bound.
No kernel may reach another device: no remote copies, remote signals or barrier semaphores. Data moves between devices by JAX's collectives and lax.ppermute only.
A program may use at most 128 MiB of HBM per device.

```python
import math
import jax
import jax.numpy as jnp
from jax import lax

D = 1536
HEADS = 24
HEAD_DIM = 64
FF = 6144
ROWS_DEV = 128
SLOTS = 5
VIEWS = 32
STRIPS = 8
VIEW_TOKENS = 1024
CAP = 2


def draw_tokens(key, part):
    keys = jax.random.split(jax.random.fold_in(key, 7), 3)
    row_scale = jnp.exp(jax.random.uniform(keys[0], (VIEWS, VIEW_TOKENS, 1), jnp.float32, math.log(0.4), math.log(4.0)))
    col_scale = jnp.exp(jax.random.uniform(keys[1], (1, 1, D), jnp.float32, math.log(0.5), math.log(2.5)))
    base_part = jax.random.normal(keys[2], (VIEWS, VIEW_TOKENS, D), jnp.float32)
    return jnp.clip(base_part * row_scale * col_scale, -48.0, 48.0).astype(jnp.bfloat16)


def query_key_pair(key, salt_tag):
    keys = jax.random.split(jax.random.fold_in(key, salt_tag), 4)
    query_weight = jax.random.normal(keys[0], (D, D), jnp.float32) / math.sqrt(D)
    key_weight = jax.random.normal(keys[3], (D, D), jnp.float32) / math.sqrt(D)
    return (jnp.clip(query_weight, -24.0, 24.0), jnp.clip(key_weight, -24.0, 24.0))


def draw_self_query(key, part):
    return query_key_pair(key, 101)[0].astype(jnp.bfloat16)


def draw_self_key(key, part):
    return query_key_pair(key, 101)[1].astype(jnp.bfloat16)


def draw_cross_query(key, part):
    return query_key_pair(key, 202)[0].astype(jnp.bfloat16)


def draw_cross_key(key, part):
    return query_key_pair(key, 202)[1].astype(jnp.bfloat16)


def draw_source_ids(key, part):
    keys = jax.random.split(jax.random.fold_in(key, 303), 2)
    positions = (VIEWS - 1) * CAP
    view_keys = jax.random.split(keys[0], VIEWS)
    shuffled = jax.vmap(lambda one_key: jax.random.permutation(one_key, positions))(view_keys)
    entry_pos = shuffled[:, :STRIPS * SLOTS].astype(jnp.int32)
    offset = entry_pos // CAP
    dest_view = jnp.arange(VIEWS, dtype=jnp.int32)[:, None]
    source_view = (dest_view + 1 + offset) % VIEWS
    source_strip = jax.random.randint(keys[1], (VIEWS, STRIPS * SLOTS), 0, STRIPS, jnp.int32)
    return (source_view * STRIPS + source_strip).reshape(VIEWS, STRIPS, SLOTS).astype(jnp.int32)


def draw_source_count(key, part):
    keys = jax.random.split(jax.random.fold_in(key, 404), 2)
    counted = jax.random.randint(keys[0], (VIEWS, STRIPS), 2, SLOTS + 1, jnp.int32)
    full_strip = jax.random.randint(keys[1], (VIEWS, 1), 0, STRIPS, jnp.int32)
    strip_index = jnp.arange(STRIPS, dtype=jnp.int32)[None, :]
    return jnp.where(strip_index == full_strip, SLOTS, counted).astype(jnp.int32)


def block_levels(stream_key, extent, shards, low, largest):
    def one(axis_at, parts):
        draws = jax.random.uniform(jax.random.fold_in(jax.random.fold_in(stream_key, 6), axis_at), (parts,), jnp.float32, low / len(shards), largest / len(shards))
        return jnp.repeat(jnp.exp(draws), extent[axis_at] // parts).reshape((-1,) + (1,) * (len(extent) - axis_at - 1))

    level = one(*shards[0])
    for cut in shards[1:]:
        level = level * one(*cut)
    return level


def gaussian(own_key, extent, deviation, reach, cuts=(), held_as=jnp.bfloat16):
    factor_of = block_levels(own_key, extent, cuts, -0.22, 0.18) if cuts else 1.0
    entries = jax.random.normal(own_key, extent, jnp.float32) * deviation * factor_of
    return jnp.minimum(jnp.maximum(entries, -reach), reach).astype(held_as)


def setup_inputs(seed: int = 0) -> dict:
    key_list = jax.random.split(jax.random.key(seed), 14)
    return {
        "tokens": draw_tokens(jax.random.fold_in(key_list[13], 71), 0),
        "source_ids": draw_source_ids(jax.random.fold_in(key_list[13], 71), 0),
        "source_count": draw_source_count(jax.random.fold_in(key_list[13], 71), 0),
        "self_query": draw_self_query(jax.random.fold_in(key_list[13], 71), 0),
        "self_key": draw_self_key(jax.random.fold_in(key_list[13], 71), 0),
        "self_value": gaussian(key_list[5], (D, D), D ** -0.5, 0.15625, ((1, 8),)),
        "self_out": gaussian(key_list[6], (D, D), 0.2, 1.1953125, ((0, 8),)),
        "cross_query": draw_cross_query(jax.random.fold_in(key_list[13], 71), 0),
        "cross_key": draw_cross_key(jax.random.fold_in(key_list[13], 71), 0),
        "cross_value": gaussian(key_list[9], (D, D), D ** -0.5, 0.15625, ((1, 8),)),
        "cross_out": gaussian(key_list[10], (D, D), 0.2, 1.1953125, ((0, 8),)),
        "mlp_up": gaussian(key_list[11], (D, FF), D ** -0.5, 0.15625, ((1, 8),)),
        "mlp_down": gaussian(key_list[12], (FF, D), FF ** -0.5, 0.078125, ((0, 8),)),
    }


def rms_rows(values_in):
    widened = values_in.astype(jnp.float32)
    scaled = widened * lax.rsqrt(lax.optimization_barrier(jnp.mean(widened * widened, axis=-1, keepdims=True)) + 1e-06)
    return scaled.astype(jnp.bfloat16)

def project_bf(normed, weight):
    return jnp.dot(normed, weight, preferred_element_type=jnp.float32).astype(jnp.bfloat16)

def attend_heads(query_heads, key_heads, value_heads, key_mask):
    scale = 1.0 / math.sqrt(HEAD_DIM)
    scores = jnp.einsum('qhe,khe->hqk', query_heads.astype(jnp.float32), key_heads.astype(jnp.float32)) * scale
    scores = jnp.where(key_mask[None, None, :], scores, -1e+30)
    weights = jax.nn.softmax(scores, axis=-1).astype(jnp.bfloat16)
    mixed_heads = jnp.einsum('hqk,khe->qhe', weights.astype(jnp.float32), value_heads.astype(jnp.float32))
    return mixed_heads.reshape(mixed_heads.shape[0], -1).astype(jnp.bfloat16)

def reference(tokens, source_ids, source_count, self_query, self_key, self_value, self_out, cross_query, cross_key, cross_value, cross_out, mlp_up, mlp_down):
    normed_all = rms_rows(tokens)
    cross_keys_all = lax.map(lambda view_rows: project_bf(view_rows, cross_key), normed_all).reshape(VIEWS * STRIPS, ROWS_DEV, D)
    cross_values_all = lax.map(lambda view_rows: project_bf(view_rows, cross_value), normed_all).reshape(VIEWS * STRIPS, ROWS_DEV, D)
    slot_index = jnp.arange(SLOTS).astype(jnp.int32)

    def one_view(view_index):
        view_rows = normed_all[view_index]
        head_shape = (VIEW_TOKENS, HEADS, HEAD_DIM)
        self_mix = attend_heads(project_bf(view_rows, self_query).reshape(head_shape), project_bf(view_rows, self_key).reshape(head_shape), project_bf(view_rows, self_value).reshape(head_shape), jnp.ones((VIEW_TOKENS,), dtype=bool))
        entry_ids = source_ids[view_index].reshape(-1).astype(jnp.int32)
        picked_keys = cross_keys_all[entry_ids].reshape(STRIPS, SLOTS * ROWS_DEV, HEADS, HEAD_DIM)
        picked_values = cross_values_all[entry_ids].reshape(STRIPS, SLOTS * ROWS_DEV, HEADS, HEAD_DIM)
        key_valid = jnp.repeat(slot_index[None, :] < source_count[view_index][:, None], ROWS_DEV, axis=1)
        cross_heads = project_bf(view_rows, cross_query).reshape(STRIPS, ROWS_DEV, HEADS, HEAD_DIM)
        cross_mix = jax.vmap(attend_heads)(cross_heads, picked_keys, picked_values, key_valid).reshape(VIEW_TOKENS, D)
        hidden = jax.nn.gelu(jnp.dot(view_rows, mlp_up, preferred_element_type=jnp.float32)).astype(jnp.bfloat16)
        branch_total = jnp.dot(self_mix, self_out, preferred_element_type=jnp.float32)
        branch_total = branch_total + jnp.dot(cross_mix, cross_out, preferred_element_type=jnp.float32)
        branch_total = branch_total + jnp.dot(hidden, mlp_down, preferred_element_type=jnp.float32)
        return (tokens[view_index].astype(jnp.float32) + branch_total).astype(jnp.bfloat16)
    return lax.map(one_view, jnp.arange(VIEWS).astype(jnp.int32))
```

```python
import math

import jax
import jax.numpy as jnp
from jax import lax
from jax.experimental import pallas as pl
from jax.experimental.pallas import tpu as pltpu
from jax.sharding import PartitionSpec as P

HEAD_DIM = 64
SLOTS = 5
GROUP = 2 * HEAD_DIM
SCALE_LOG2 = math.log2(math.e) / math.sqrt(HEAD_DIM)
BF16 = jnp.bfloat16
F32 = jnp.float32


def rms_rows(values_in):
    widened = values_in.astype(F32)
    scaled = widened * lax.rsqrt(jnp.mean(widened * widened, axis=-1, keepdims=True) + 1e-06)
    return scaled.astype(BF16)


def ring_pairs(size, step):
    return [(i, (i + step) % size) for i in range(size)]


def shift(value, size, step):
    return lax.ppermute(value, "strip", ring_pairs(size, step))


def ring_gather(blocks, size):
    far = size // 2
    ahead, behind = list(blocks), list(blocks)
    found = [{0: block} for block in blocks]
    for step in range(1, far):
        for i in range(len(blocks)):
            ahead[i] = shift(ahead[i], size, 1)
            behind[i] = shift(behind[i], size, -1)
            found[i][size - step] = ahead[i]
            found[i][step] = behind[i]
    for i in range(len(blocks)):
        half = blocks[i].shape[0] // 2
        first = shift(ahead[i][:half], size, 1)
        second = shift(behind[i][half:], size, -1)
        found[i][far] = jnp.concatenate([first, second], 0)
    return [[entry[j] for j in range(size)] for entry in found]


def ring_reduce(parts, size):
    far = size // 2
    half = parts[0].shape[0] // 2

    def add(received, part):
        return (received.astype(F32) + part.astype(F32)).astype(BF16)

    top = shift(parts[far][:half], size, 1)
    low = shift(parts[far][half:], size, -1)
    ahead = jnp.concatenate([add(top, parts[far - 1][:half]), parts[far - 1][half:]], 0)
    behind = jnp.concatenate([parts[size - far + 1][:half], add(low, parts[size - far + 1][half:])], 0)
    for step in range(far - 1, 0, -1):
        ahead = shift(ahead, size, 1)
        behind = shift(behind, size, -1)
        if step > 1:
            ahead = add(ahead, parts[step - 1])
            behind = add(behind, parts[size - step + 1])
    return ahead, behind


def pair_heads(keys, values):
    pieces = []
    for at in range(0, keys.shape[1], HEAD_DIM):
        pieces += [keys[:, at : at + HEAD_DIM], values[:, at : at + HEAD_DIM]]
    return jnp.concatenate(pieces, 1).astype(BF16)


def pad_heads(queries):
    return pair_heads(queries, jnp.zeros_like(queries))


def dot(a, b):
    return jnp.dot(a, b, preferred_element_type=F32)


def dot_rows(a, b):
    return lax.dot_general(a, b, (((1,), (1,)), ((), ())), preferred_element_type=F32)


def pack_kernel(table, x_ref, key_ref, value_ref, out_ref, held):
    step = pl.program_id(0)
    rows = held.shape[1]

    @pl.when(step == 0)
    def _():
        for at in range(0, held.shape[0], 2):
            block = x_ref[at : at + 2].reshape(2 * rows, x_ref.shape[2])
            paired = pair_heads(dot(block, key_ref[...]), dot(block, value_ref[...]))
            held[at : at + 2] = paired.reshape(2, rows, held.shape[2])

    for i in range(out_ref.shape[0]):
        out_ref[i] = held[table[step * out_ref.shape[0] + i]]


def pack_items(table, gathered, weight_key, weight_value):
    strips, rows, width = gathered.shape
    cols = weight_key.shape[1]
    items = table.shape[0]
    block = items // 4
    whole = lambda *shape: pl.BlockSpec(shape, lambda i, t: (0,) * len(shape))
    return pl.pallas_call(
        pack_kernel,
        grid_spec=pltpu.PrefetchScalarGridSpec(
            num_scalar_prefetch=1,
            grid=(items // block,),
            in_specs=[whole(strips, rows, width), whole(width, cols), whole(width, cols)],
            out_specs=pl.BlockSpec((block, rows, 2 * cols), lambda i, t: (i, 0, 0)),
            scratch_shapes=[pltpu.VMEM((strips, rows, 2 * cols), BF16)],
        ),
        out_shape=jax.ShapeDtypeStruct((items, rows, 2 * cols), BF16),
        name="pack_items",
    )(table, gathered, weight_key, weight_value)


def project_kernel(x_ref, sq, sk, sv, cq, up, self_q, self_kv, cross_q, hidden):
    x = x_ref[...].reshape(self_q.shape[0], x_ref.shape[2])
    self_q[...] = pad_heads(dot(x, sq[...]))
    self_kv[...] = pair_heads(dot(x, sk[...]), dot(x, sv[...]))
    cross_q[...] = pad_heads(dot(x, cq[...]))
    hidden[...] = jax.nn.gelu(dot(x, up[...])).astype(BF16)


def project(gathered, sq, sk, sv, cq, up):
    strips, rows, width = gathered.shape
    cols, ff = sq.shape[1], up.shape[1]
    per = 2
    whole = lambda array: pl.BlockSpec(array.shape, lambda i: (0, 0))
    out = lambda n: pl.BlockSpec((per * rows, n), lambda i: (i, 0))
    shape = lambda n: jax.ShapeDtypeStruct((strips * rows, n), BF16)
    return pl.pallas_call(
        project_kernel,
        grid=(strips // per,),
        in_specs=[pl.BlockSpec((per, rows, width), lambda i: (i, 0, 0))]
        + [whole(w) for w in (sq, sk, sv, cq, up)],
        out_specs=[out(2 * cols), out(2 * cols), out(2 * cols), out(ff)],
        out_shape=[shape(2 * cols), shape(2 * cols), shape(2 * cols), shape(ff)],
        name="project",
    )(gathered, sq, sk, sv, cq, up)


def self_kernel(q_ref, kv_ref, out_ref):
    mixes = []
    for at in range(0, q_ref.shape[1], GROUP):
        pairs = kv_ref[:, at : at + GROUP]
        scores = dot_rows(q_ref[:, at : at + GROUP], pairs)
        top = jnp.max(scores, axis=1, keepdims=True)
        weights = jnp.exp2((scores - top) * SCALE_LOG2)
        total = jnp.sum(weights, axis=1, keepdims=True)
        mix = dot(weights.astype(BF16), pairs)
        mixes.append(mix[:, HEAD_DIM:] / total)
    out_ref[...] = jnp.concatenate(mixes, 1).astype(BF16)


def self_attention(q, kv):
    rows, width = q.shape
    block = 256
    return pl.pallas_call(
        self_kernel,
        grid=(rows // block,),
        in_specs=[
            pl.BlockSpec((block, width), lambda i: (i, 0)),
            pl.BlockSpec((rows, width), lambda i: (0, 0)),
        ],
        out_specs=pl.BlockSpec((block, width // 2), lambda i: (i, 0)),
        out_shape=jax.ShapeDtypeStruct((rows, width // 2), BF16),
        name="self_attention",
    )(q, kv)


def cross_kernel(items, counts, me, q_ref, *refs):
    item_refs, out_ref = refs[:-1], refs[-1]
    count = counts[pl.program_id(0)]
    mixes = []
    for at in range(0, q_ref.shape[1], GROUP):
        queries = q_ref[:, at : at + GROUP]
        scores = []
        for k, item in enumerate(item_refs):
            score = dot_rows(queries, item[0, :, at : at + GROUP])
            scores.append(jnp.where(k < count, score, -1e30))
        top = scores[0]
        for score in scores[1:]:
            top = jnp.maximum(top, score)
        top = jnp.max(top, axis=1, keepdims=True)
        total, mix = 0.0, 0.0
        for score, item in zip(scores, item_refs):
            weights = jnp.exp2((score - top) * SCALE_LOG2)
            total = total + weights
            mix = mix + dot(weights.astype(BF16), item[0, :, at : at + GROUP])
        total = jnp.sum(total, axis=1, keepdims=True)
        mixes.append(mix[:, HEAD_DIM:] / total)
    out_ref[0] = jnp.concatenate(mixes, 1).astype(BF16)


def cross_attention(items, counts, me, q, received, strips):
    rows = q.shape[0] // strips
    width = q.shape[1]

    def item_spec(k):
        return pl.BlockSpec((1, rows, width), lambda j, t, c, m: (t[j * SLOTS + k], 0, 0))

    return pl.pallas_call(
        cross_kernel,
        grid_spec=pltpu.PrefetchScalarGridSpec(
            num_scalar_prefetch=3,
            grid=(strips,),
            in_specs=[pl.BlockSpec((rows, width), lambda j, t, c, m: (j, 0))]
            + [item_spec(k) for k in range(SLOTS)],
            out_specs=pl.BlockSpec(
                (1, rows, width // 2), lambda j, t, c, m: (lax.rem(m[0] + j, strips), 0, 0)
            ),
        ),
        out_shape=jax.ShapeDtypeStruct((strips, rows, width // 2), BF16),
        name="cross_attention",
    )(items, counts, me, q, *([received] * SLOTS))


def finish_kernel(place, mix_ref, mine_ref, other_ref, token_ref, ahead_ref, behind_ref, own_ref, out_ref):
    me, side = place[0], place[1]
    strips = mix_ref.shape[0]
    half = out_ref.shape[1] // 2
    for weights, part in ((mine_ref, side), (other_ref, 1 - side)):
        total = 0.0
        for j in range(strips):
            total = total + dot(mix_ref[lax.rem(me + j, strips)], weights[j])
        cols = pl.ds(pl.multiple_of(part * half, 128), half)
        early = ahead_ref[:, cols].astype(F32) + behind_ref[:, cols].astype(F32) + own_ref[:, cols].astype(F32)
        out_ref[:, cols] = (token_ref[:, cols].astype(F32) + (total + early)).astype(BF16)


def finish(place, mix, mine, other, token_rows, ahead, behind, own):
    operands = (mix, mine, other, token_rows, ahead, behind, own)
    whole = lambda array: pl.BlockSpec(array.shape, lambda i, p: (0,) * array.ndim)
    return pl.pallas_call(
        finish_kernel,
        grid_spec=pltpu.PrefetchScalarGridSpec(
            num_scalar_prefetch=1,
            grid=(1,),
            in_specs=[whole(a) for a in operands],
            out_specs=whole(token_rows),
        ),
        out_shape=jax.ShapeDtypeStruct(token_rows.shape, BF16),
        name="finish",
    )(place, *operands)


def routing(source_ids, source_count, my_view, my_strip, n_view, n_strip, capacity):
    flat_ids = source_ids.reshape(n_view, -1)
    source_view = flat_ids // n_strip
    source_strip = flat_ids % n_strip
    order = jnp.arange(flat_ids.shape[1], dtype=jnp.int32)
    earlier = order[None, :] < order[:, None]
    same_view = source_view[:, :, None] == source_view[:, None, :]
    rank = jnp.sum(jnp.logical_and(same_view, earlier[None]), axis=2)
    slots = jnp.arange(capacity, dtype=jnp.int32)
    match = jnp.logical_and(
        (source_view == my_view)[:, :, None], rank[:, :, None] == slots[None, None, :]
    )
    strip_of_slot = jnp.sum(jnp.where(match, source_strip[:, :, None], 0), axis=1)
    table = (strip_of_slot - my_strip + n_strip) % n_strip
    mine = lambda array: lax.dynamic_index_in_dim(array, my_view, 0, keepdims=False)
    items = (mine(source_view) * capacity + mine(rank)).reshape(n_strip, SLOTS)
    items = jnp.roll(items, -my_strip, 0).reshape(-1)
    counts = jnp.roll(mine(source_count), -my_strip, 0)
    return table.reshape(-1).astype(jnp.int32), items.astype(jnp.int32), counts.astype(jnp.int32)


def per_device(
    tokens,
    source_ids,
    source_count,
    self_query,
    self_key,
    self_value,
    self_out,
    cross_query,
    cross_key,
    cross_value,
    cross_out,
    mlp_up,
    mlp_down,
):
    n_view = lax.axis_size("view")
    n_strip = lax.axis_size("strip")
    my_view = lax.axis_index("view")
    my_strip = lax.axis_index("strip")
    side = my_view % 2
    rows = tokens.shape[1]
    capacity = (n_strip * SLOTS + n_view - 2) // (n_view - 1)
    table, items, counts = routing(
        source_ids, source_count, my_view, my_strip, n_view, n_strip, capacity
    )

    normed = rms_rows(tokens[0])
    top, low = ring_gather([normed[: rows // 2], normed[rows // 2 :]], n_strip)
    gathered = jnp.stack([jnp.concatenate([a, b], 0) for a, b in zip(top, low)])

    outgoing = pack_items(table, gathered, cross_key, cross_value)
    outgoing = outgoing.reshape(n_view, capacity, rows, outgoing.shape[-1])
    received = lax.all_to_all(outgoing, "view", split_axis=0, concat_axis=0, tiled=True)
    received = received.reshape(n_view * capacity, rows, outgoing.shape[-1])

    half = cross_out.shape[1] // 2
    my_half = lax.dynamic_slice_in_dim(cross_out, side * half, half, 1)
    my_halves = jnp.stack(ring_gather([my_half], n_strip)[0])
    other_halves = lax.ppermute(my_halves, "view", [(i, i ^ 1) for i in range(n_view)])

    self_q, self_kv, cross_q, hidden = project(
        gathered, self_query, self_key, self_value, cross_query, mlp_up
    )
    self_mix = self_attention(self_q, self_kv)
    early = (dot(self_mix, self_out) + dot(hidden, mlp_down)).astype(BF16)
    early = early.reshape(n_strip, rows, early.shape[-1])
    ahead, behind = ring_reduce([early[j] for j in range(n_strip)], n_strip)

    cross_mix = cross_attention(
        items, counts, my_strip.reshape(1).astype(jnp.int32), cross_q, received, n_strip
    )
    cross_mix = lax.all_to_all(cross_mix, "strip", split_axis=0, concat_axis=0, tiled=True)
    place = jnp.stack([my_strip, side]).astype(jnp.int32)
    return finish(place, cross_mix, my_halves, other_halves, tokens[0], ahead, behind, early[0])[None]


def solution(mesh):
    in_specs = (
        P("view", "strip", None),
        P(),
        P(),
        P(None, "strip"),
        P(None, "strip"),
        P(None, "strip"),
        P("strip", None),
        P(None, "strip"),
        P(None, "strip"),
        P(None, "strip"),
        P("strip", None),
        P(None, "strip"),
        P("strip", None),
    )
    out_specs = P("view", "strip", None)
    return jax.shard_map(
        per_device, mesh=mesh, in_specs=in_specs, out_specs=out_specs, check_vma=False
    )
```

```python
import math

import jax
import jax.numpy as jnp
from jax import lax
from jax.experimental import pallas as pl
from jax.experimental.pallas import tpu as pltpu
from jax.sharding import PartitionSpec as P


HEAD_DIM = 64
SLOTS = 5
GROUP = 2 * HEAD_DIM
SCALE_LOG2 = math.log2(math.e) / math.sqrt(HEAD_DIM)
BF16 = jnp.bfloat16
F32 = jnp.float32


def rms_rows(values_in):
    widened = values_in.astype(F32)
    scaled = widened * lax.rsqrt(jnp.mean(widened * widened, axis=-1, keepdims=True) + 1e-06)
    return scaled.astype(BF16)


def ring_pairs(size, step):
    return [(i, (i + step) % size) for i in range(size)]


def shift(value, size, step):
    return lax.ppermute(value, "strip", ring_pairs(size, step))


def pair_heads(keys, values):
    pieces = []
    for at in range(0, keys.shape[1], HEAD_DIM):
        pieces += [keys[:, at : at + HEAD_DIM], values[:, at : at + HEAD_DIM]]
    return jnp.concatenate(pieces, 1).astype(BF16)


def pad_heads(queries):
    return pair_heads(queries, jnp.zeros_like(queries))


def dot(a, b):
    return jnp.dot(a, b, preferred_element_type=F32)


def dot_rows(a, b):
    return lax.dot_general(a, b, (((1,), (1,)), ((), ())), preferred_element_type=F32)


def slot_of(strip):
    paired = jnp.where(strip < 4, 2 * strip - 1, 2 * (7 - strip))
    return jnp.where(strip == 0, 6, jnp.where(strip == 4, 7, paired))


OFFSETS = (7, 1, 6, 2, 5, 3, 0, 4)


def whole(array):
    return pl.BlockSpec(array.shape, lambda *_: (0,) * array.ndim)


def project_rows(x, weights, outs):
    sq, sk, sv, cq, up, ck, cv = weights
    self_q, self_kv, cross_q, hidden = outs[:4]
    if ck is not None:
        outs[4][0] = pair_heads(dot_rows(x, ck[...]), dot_rows(x, cv[...]))
    self_kv[0] = pair_heads(dot_rows(x, sk[...]), dot_rows(x, sv[...]))
    self_q[0] = pad_heads(dot_rows(x, sq[...]))
    cross_q[0] = pad_heads(dot_rows(x, cq[...]))
    hidden[0] = jax.nn.gelu(dot(x, up[...])).astype(BF16)


def project(blocks, weights, held, place, with_cross):
    sq, sk, sv, cq, up, ck, cv = weights
    operands = [*blocks, sq, sk, sv, cq, up] + ([ck, cv] if with_cross else [])
    count = len(blocks)
    rows = sum(block.shape[0] for block in blocks)
    cols, ff = sq.shape[0], up.shape[1]
    widths = [2 * cols, 2 * cols, 2 * cols, ff] + ([2 * cols] if with_cross else [])
    n_held = 0 if held is None else len(held)

    def kernel(*refs):
        x = jnp.concatenate([ref[...] for ref in refs[:count]], 0)
        inputs = list(refs[count : len(operands)])
        if not with_cross:
            inputs += [None, None]
        project_rows(x, inputs, refs[len(operands) + n_held :])

    depth = 4
    return pl.pallas_call(
        kernel,
        grid=(1,),
        in_specs=[whole(a) for a in operands] + [pl.BlockSpec(memory_space=pl.ANY)] * n_held,
        out_specs=[pl.BlockSpec((1, rows, n), lambda i: (place, 0, 0)) for n in widths],
        out_shape=[jax.ShapeDtypeStruct((depth, rows, n), BF16) for n in widths],
        input_output_aliases={len(operands) + i: i for i in range(n_held)},
        name="project",
    )(*operands, *([] if held is None else held))


def pack_items(table, blocks, paired, ck, cv, capacity):
    count = len(blocks)
    depth, both, width = paired.shape
    rows = both // 2
    items = table.shape[0]
    n_view = items // capacity
    steps = 4
    block = n_view // steps

    def kernel(table_ref, *refs):
        xs, (pair_ref, ck_ref, cv_ref, out_ref, held) = refs[:count], refs[count:]
        step = pl.program_id(0)

        @pl.when(step == 0)
        def _():
            x = jnp.concatenate([ref[...] for ref in xs], 0)
            last = pair_heads(dot_rows(x, ck_ref[...]), dot_rows(x, cv_ref[...]))
            held[2 * depth - 2] = last[:rows]
            held[2 * depth - 1] = last[rows:]
            for k in range(depth - 1):
                held[2 * k] = pair_ref[k, :rows]
                held[2 * k + 1] = pair_ref[k, rows:]

        for i in range(block):
            for j in range(capacity):
                out_ref[i, j] = held[table_ref[j * n_view + step * block + i]]

    return pl.pallas_call(
        kernel,
        grid_spec=pltpu.PrefetchScalarGridSpec(
            num_scalar_prefetch=1,
            grid=(steps,),
            in_specs=[whole(x) for x in blocks]
            + [pl.BlockSpec((depth - 1, both, width), lambda i, t: (0, 0, 0)), whole(ck), whole(cv)],
            out_specs=pl.BlockSpec((block, capacity, rows, width), lambda i, t: (i, 0, 0, 0)),
            scratch_shapes=[pltpu.VMEM((2 * depth, rows, width), BF16)],
        ),
        out_shape=jax.ShapeDtypeStruct((n_view, capacity, rows, width), BF16),
        name="pack_items",
    )(table, *blocks, paired, ck, cv)


def early_kernel(q_ref, kv_ref, hidden_ref, out_w, down_w, result):
    mixes = []
    for at in range(0, q_ref.shape[2], GROUP):
        pairs = kv_ref[:, at : at + GROUP]
        scores = dot_rows(q_ref[0, :, at : at + GROUP], pairs)
        top = jnp.max(scores, axis=1, keepdims=True)
        weights = jnp.exp2((scores - top) * SCALE_LOG2)
        total = jnp.sum(weights, axis=1, keepdims=True)
        mix = dot(weights.astype(BF16), pairs)
        mixes.append(mix[:, HEAD_DIM:] / total)
    mix = jnp.concatenate(mixes, 1).astype(BF16)
    result[0] = (dot(mix, out_w[...]) + dot(hidden_ref[0], down_w[...])).astype(BF16)


def early_terms(q, kv, hidden, out_w, down_w, first, count):
    depth, rows, width = q.shape
    kv = kv.reshape(depth * rows, width)
    ff, cols = hidden.shape[2], out_w.shape[1]
    return pl.pallas_call(
        early_kernel,
        grid=(count,),
        in_specs=[
            pl.BlockSpec((1, rows, width), lambda i: (first + i, 0, 0)),
            whole(kv),
            pl.BlockSpec((1, rows, ff), lambda i: (first + i, 0, 0)),
            whole(out_w),
            whole(down_w),
        ],
        out_specs=pl.BlockSpec((1, rows, cols), lambda i: (i, 0, 0)),
        out_shape=jax.ShapeDtypeStruct((count, rows, cols), BF16),
        name="early_terms",
    )(q, kv, hidden, out_w, down_w)


def add_pair(ahead, behind, terms, at):
    rows = terms.shape[1] // 2

    def kernel(ahead_ref, behind_ref, term_ref, ahead_out, behind_out):
        def add(received, term):
            return (received.astype(F32) + term.astype(F32)).astype(BF16)

        if ahead.shape[0] < rows:
            n = ahead.shape[0]
            ahead_out[:n] = add(ahead_ref[...], term_ref[0, rows : rows + n])
            ahead_out[n:] = term_ref[0, rows + n :]
            behind_out[:n] = term_ref[0, :n]
            behind_out[n:] = add(behind_ref[...], term_ref[0, n:rows])
        else:
            ahead_out[...] = add(ahead_ref[...], term_ref[0, rows:])
            behind_out[...] = add(behind_ref[...], term_ref[0, :rows])

    shape = jax.ShapeDtypeStruct((rows, terms.shape[2]), BF16)
    return pl.pallas_call(
        kernel,
        grid=(1,),
        in_specs=[whole(ahead), whole(behind), pl.BlockSpec((1, *terms.shape[1:]), lambda i: (at, 0, 0))],
        out_specs=[pl.BlockSpec(shape.shape, lambda i: (0, 0))] * 2,
        out_shape=[shape, shape],
        name="add_pair",
    )(ahead, behind, terms)


def cross_attention(items, counts, me, q, received, strips):
    rows, width = received.shape[1:]
    heads = width // GROUP

    def kernel(item_ref, count_ref, me_ref, q_ref, received_ref, out_ref, held, sems):
        def strip_at(place):
            offset = OFFSETS[0]
            for k in range(1, strips):
                offset = jnp.where(place == k, OFFSETS[k], offset)
            return lax.rem(me_ref[0] + offset, strips)

        def copies(place):
            strip = strip_at(place)
            return [
                pltpu.make_async_copy(
                    received_ref.at[item_ref[k * strips + strip]],
                    held.at[place, pl.ds(k * rows, rows)],
                    sems.at[place, k],
                )
                for k in range(SLOTS)
            ]

        @pl.loop(0, strips)
        def _(place):
            for copy in copies(place):
                copy.start()

        @pl.loop(0, strips)
        def _(place):
            for copy in copies(place):
                copy.wait()
            strip = strip_at(place)
            in_use = lax.broadcasted_iota(jnp.int32, (SLOTS * rows, rows), 0) < count_ref[strip] * rows
            queries = q_ref[place // 2, pl.ds(lax.rem(place, 2) * rows, rows), :]
            for head in range(heads):
                at = head * GROUP
                pairs = held[place, :, at : at + GROUP]
                scores = dot_rows(pairs, queries[:, at : at + GROUP])
                scores = jnp.where(in_use, scores, -1e30)
                top = jnp.max(scores, axis=0, keepdims=True)
                weights = jnp.exp2((scores - top) * SCALE_LOG2)
                total = jnp.sum(weights, axis=0, keepdims=True)
                mix = lax.dot_general(
                    pairs, weights.astype(BF16), (((0,), (0,)), ((), ())), preferred_element_type=F32
                )
                out_ref[strip, head * HEAD_DIM : (head + 1) * HEAD_DIM] = (
                    mix[HEAD_DIM:] / total
                ).astype(BF16)

    smem = pl.BlockSpec(memory_space=pltpu.SMEM)
    return pl.pallas_call(
        kernel,
        in_specs=[smem, smem, smem, pl.BlockSpec(memory_space=pltpu.VMEM), pl.BlockSpec(memory_space=pl.ANY)],
        out_specs=pl.BlockSpec(memory_space=pltpu.VMEM),
        out_shape=jax.ShapeDtypeStruct((strips, width // 2, rows), BF16),
        scratch_shapes=[
            pltpu.VMEM((strips, SLOTS * rows, width), BF16),
            pltpu.SemaphoreType.DMA((strips, SLOTS)),
        ],
        name="cross_attention",
    )(items, counts, me, q, received)


def collect(pieces, far):
    strips = len(pieces) + 1
    rows, cols = pieces[0].shape
    blocks = pieces[: strips // 2] + list(far) + pieces[strips // 2 :]

    def kernel(*refs):
        out_ref, at = refs[-1], 0
        for ref in refs[:-1]:
            n = ref.shape[0]
            out_ref[at // rows, at % rows : at % rows + n] = ref[...]
            at += n

    vmem = pl.BlockSpec(memory_space=pltpu.VMEM)
    return pl.pallas_call(
        kernel,
        in_specs=[vmem] * len(blocks),
        out_specs=vmem,
        out_shape=jax.ShapeDtypeStruct((strips, rows, cols), BF16),
        name="collect",
    )(*blocks)


def finish(place, mix, mine, other, token_rows, ahead, behind, terms, at):
    strips, width, half = mine.shape
    rows = token_rows.shape[0]
    cols = 256

    def kernel(place_ref, mix_ref, mine_ref, other_ref, token_ref, ahead_ref, behind_ref, own_ref, out_ref):
        me, side = place_ref[0], place_ref[1]
        step = pl.program_id(0)
        for weights, part in ((mine_ref, side), (other_ref, 1 - side)):
            total = 0.0
            for j in range(strips):
                total = total + lax.dot_general(
                    mix_ref[lax.rem(me + j, strips)],
                    weights[j],
                    (((0,), (0,)), ((), ())),
                    preferred_element_type=F32,
                )
            here = pl.ds(pl.multiple_of(part * half + step * cols, 128), cols)
            early = ahead_ref[:, here].astype(F32) + behind_ref[:, here].astype(F32)
            early = early + own_ref[0, :, here].astype(F32)
            out_ref[:, here] = (token_ref[:, here].astype(F32) + (total + early)).astype(BF16)

    return pl.pallas_call(
        kernel,
        grid_spec=pltpu.PrefetchScalarGridSpec(
            num_scalar_prefetch=1,
            grid=(half // cols,),
            in_specs=[
                whole(mix),
                pl.BlockSpec((strips, width, cols), lambda i, p: (0, 0, i)),
                pl.BlockSpec((strips, width, cols), lambda i, p: (0, 0, i)),
                whole(token_rows),
                whole(ahead),
                whole(behind),
                pl.BlockSpec((1, rows, terms.shape[2]), lambda i, p: (at, 0, 0)),
            ],
            out_specs=whole(token_rows),
        ),
        out_shape=jax.ShapeDtypeStruct(token_rows.shape, BF16),
        name="finish",
    )(place, mix, mine, other, token_rows, ahead, behind, terms)


def routing(source_ids, source_count, my_view, my_strip, n_view, n_strip):
    lists = source_ids.transpose(2, 1, 0).reshape(-1, n_view)
    order = lax.broadcasted_iota(jnp.int32, lists.shape, 0)
    keyed = order * n_strip + lists % n_strip
    match = lists // n_strip == my_view
    first = jnp.min(jnp.where(match, keyed, lists.size * n_strip), axis=0)
    last = jnp.max(jnp.where(match, keyed, -1), axis=0)
    strips = jnp.stack([first, jnp.maximum(last, 0)]) % n_strip
    table = slot_of((strips - my_strip + n_strip) % n_strip)
    mine = lax.dynamic_slice_in_dim(lists, my_view, 1, 1) // n_strip
    count = mine.shape[0]
    earlier = lax.broadcasted_iota(jnp.int32, (count, count), 0) < lax.broadcasted_iota(
        jnp.int32, (count, count), 1
    )
    again = jnp.max(jnp.where(jnp.logical_and(mine == mine.T, earlier), 1, 0), axis=0)
    items = mine[:, 0] * 2 + again
    counts = lax.dynamic_slice_in_dim(source_count, my_view, 1, 0)[0]
    return table.reshape(-1), items, counts


def per_device(
    tokens,
    source_ids,
    source_count,
    self_query,
    self_key,
    self_value,
    self_out,
    cross_query,
    cross_key,
    cross_value,
    cross_out,
    mlp_up,
    mlp_down,
):
    n_view = lax.axis_size("view")
    n_strip = lax.axis_size("strip")
    my_view = lax.axis_index("view")
    my_strip = lax.axis_index("strip")
    side = my_view % 2
    capacity = 2
    routes = routing(source_ids, source_count, my_view, my_strip, n_view, n_strip)
    table, items, counts = lax.optimization_barrier(routes)

    weights = [self_query.T, self_key.T, self_value.T, cross_query.T, mlp_up, cross_key.T, cross_value.T]

    def both(up, down):
        return shift(up, n_strip, 1), shift(down, n_strip, -1)

    normed = rms_rows(tokens[0])
    half_rows = normed.shape[0] // 2
    ahead, behind, held = normed, normed, None
    ahead, behind = both(ahead, behind)
    for step in range(3):
        pair = [ahead, behind]
        if step < 2:
            ahead, behind = both(ahead, behind)
        else:
            ahead, behind = both(ahead[:half_rows], behind[half_rows:])
        held = project(pair, weights, held, step, True)
    blocks = [normed, ahead, behind]
    outgoing = pack_items(table, blocks, held[4], weights[5], weights[6], capacity)
    received = lax.all_to_all(outgoing, "view", split_axis=0, concat_axis=0, tiled=True)
    received = received.reshape(n_view * capacity, *outgoing.shape[2:])

    half = cross_out.shape[1] // 2
    my_half = lax.dynamic_slice_in_dim(cross_out, side * half, half, 1)
    my_half, outgoing, blocks = lax.optimization_barrier((my_half, outgoing, blocks))
    ahead, behind, found = my_half, my_half, {0: my_half}
    for step in range(1, 4):
        ahead, behind = both(ahead, behind)
        found[n_strip - step], found[step] = ahead, behind
    part = my_half.shape[0] // 2
    far = both(ahead[:part], behind[part:])
    my_halves = collect([found[j] for j in range(n_strip) if j != n_strip // 2], far)
    other_halves = lax.ppermute(my_halves, "view", [(i, i ^ 1) for i in range(n_view)])

    self_q, self_kv, cross_q, hidden = project(blocks, weights, held[:4], 3, False)
    late = early_terms(self_q, self_kv, hidden, self_out, mlp_down, 2, 2)
    soon = early_terms(self_q, self_kv, hidden, self_out, mlp_down, 0, 2)
    rows = normed.shape[0]
    ahead, behind = both(late[1, rows : rows + half_rows], late[1, rows + half_rows :])
    for terms, at in ((late, 0), (soon, 1), (soon, 0)):
        ahead, behind = add_pair(ahead, behind, terms, at)
        ahead, behind = both(ahead, behind)

    place = jnp.stack([my_strip, side]).astype(jnp.int32)
    cross_mix = cross_attention(items, counts, place[:1], cross_q, received, n_strip)
    cross_mix = lax.all_to_all(cross_mix, "strip", split_axis=0, concat_axis=0, tiled=True)
    return finish(place, cross_mix, my_halves, other_halves, tokens[0], ahead, behind, late, 1)[None]


def solution(mesh):
    in_specs = (
        P("view", "strip", None),
        P(),
        P(),
        P(None, "strip"),
        P(None, "strip"),
        P(None, "strip"),
        P("strip", None),
        P(None, "strip"),
        P(None, "strip"),
        P(None, "strip"),
        P("strip", None),
        P(None, "strip"),
        P("strip", None),
    )
    out_specs = P("view", "strip", None)

    return jax.shard_map(
        per_device, mesh=mesh, in_specs=in_specs, out_specs=out_specs, check_vma=False
    )
```

```python
import math

import jax
import jax.numpy as jnp
from jax import lax
from jax.experimental import pallas as pl
from jax.experimental.pallas import tpu as pltpu
from jax.sharding import PartitionSpec as P


HEAD_DIM = 64
SLOTS = 5
GROUP = 2 * HEAD_DIM
SCALE_LOG2 = math.log2(math.e) / math.sqrt(HEAD_DIM)
BF16 = jnp.bfloat16
F32 = jnp.float32


def rms_rows(values_in):
    widened = values_in.astype(F32)
    scaled = widened * lax.rsqrt(jnp.mean(widened * widened, axis=-1, keepdims=True) + 1e-06)
    return scaled.astype(BF16)


def ring_pairs(size, step):
    return [(i, (i + step) % size) for i in range(size)]


def shift(value, size, step):
    return lax.ppermute(value, "strip", ring_pairs(size, step))


def pair_heads(keys, values):
    pieces = []
    for at in range(0, keys.shape[1], HEAD_DIM):
        pieces += [keys[:, at : at + HEAD_DIM], values[:, at : at + HEAD_DIM]]
    return jnp.concatenate(pieces, 1).astype(BF16)


def pad_heads(queries):
    return pair_heads(queries, jnp.zeros_like(queries))


def params(mebibytes):
    return pltpu.CompilerParams(vmem_limit_bytes=mebibytes << 20)


def split(array, at, first, count):
    half = count // 2

    def kernel(ref, top_ref, low_ref):
        block = ref.at[at] if array.ndim == 3 else ref
        top_ref[...] = block[first : first + half]
        low_ref[...] = block[first + half : first + count]

    vmem = pl.BlockSpec(memory_space=pltpu.VMEM)
    return pl.pallas_call(
        kernel,
        in_specs=[vmem],
        out_specs=[vmem, vmem],
        out_shape=[jax.ShapeDtypeStruct((half, array.shape[-1]), BF16)] * 2,
        compiler_params=params(12),
        name="split",
    )(array)


def dot(a, b):
    return jnp.dot(a, b, preferred_element_type=F32)


def dot_rows(a, b):
    return lax.dot_general(a, b, (((1,), (1,)), ((), ())), preferred_element_type=F32)


def slot_of(strip):
    paired = jnp.where(strip < 4, 2 * strip - 1, 2 * (7 - strip))
    return jnp.where(strip == 0, 6, jnp.where(strip == 4, 7, paired))


OFFSETS = (7, 1, 6, 2, 5, 3, 0, 4)


def whole(array):
    return pl.BlockSpec(array.shape, lambda *_: (0,) * array.ndim)


def project_rows(x, weights, outs):
    sq, sk, sv, cq, up, ck, cv = weights
    self_q, self_kv, cross_q, hidden = outs[:4]

    def put(out, value):
        out[...] = value.reshape(out.shape)

    if ck is not None:
        put(outs[4], pair_heads(dot_rows(x, ck[...]), dot_rows(x, cv[...])))
    put(self_kv, pair_heads(dot_rows(x, sk[...]), dot_rows(x, sv[...])))
    put(self_q, pad_heads(dot_rows(x, sq[...])))
    put(cross_q, pad_heads(dot_rows(x, cq[...])))
    put(hidden, jax.nn.gelu(dot(x, up[...])).astype(BF16))


def project(blocks, weights, held, place, with_cross):
    sq, sk, sv, cq, up, ck, cv = weights
    operands = [*blocks, sq, sk, sv, cq, up] + ([ck, cv] if with_cross else [])
    count = len(blocks)
    depth, both = 4, 2 * blocks[0].shape[0]
    per = sum(block.shape[0] for block in blocks) // both
    cols, ff = sq.shape[0], up.shape[1]
    widths = [2 * cols, 2 * cols, 2 * cols, ff] + ([2 * cols] if with_cross else [])
    n_held = 0 if held is None else len(held)

    def kernel(*refs):
        x = jnp.concatenate([ref[...] for ref in refs[:count]], 0)
        inputs = list(refs[count : len(operands)])
        if not with_cross:
            inputs += [None, None]
        project_rows(x, inputs, refs[len(operands) + n_held :])

    return pl.pallas_call(
        kernel,
        grid=(1,),
        in_specs=[whole(a) for a in operands] + [pl.BlockSpec(memory_space=pl.ANY)] * n_held,
        out_specs=[pl.BlockSpec((per, both, n), lambda i: (place, 0, 0)) for n in widths],
        out_shape=[jax.ShapeDtypeStruct((depth, both, n), BF16) for n in widths],
        input_output_aliases={len(operands) + i: i for i in range(n_held)},
        name="project",
    )(*operands, *([] if held is None else held))


def cross_pairs(blocks, ck, cv, paired):
    rows = blocks[0].shape[0]
    _, both, width = paired.shape

    def kernel(up_ref, down_ref, own_ref, ck_ref, cv_ref, _, out_ref):
        x = jnp.concatenate([up_ref[...], down_ref[...], own_ref[...]], 0)
        last = pair_heads(dot_rows(x, ck_ref[...]), dot_rows(x, cv_ref[...]))
        out_ref[0] = last[:both]
        out_ref[1, :rows] = last[both:]
        out_ref[1, rows:] = jnp.zeros((rows, width), BF16)

    operands = (*blocks, ck, cv)
    return pl.pallas_call(
        kernel,
        grid=(1,),
        in_specs=[whole(a) for a in operands] + [pl.BlockSpec(memory_space=pl.ANY)],
        out_specs=pl.BlockSpec((2, both, width), lambda i: (1, 0, 0)),
        out_shape=jax.ShapeDtypeStruct(paired.shape, BF16),
        input_output_aliases={len(operands): 0},
        name="cross_pairs",
    )(*operands, paired)


def pack_items(table, far, paired, ck, cv, n_view, capacity):
    depth, both, width = paired.shape
    rows = both // 2
    steps = 8
    block = n_view // steps

    def kernel(table_ref, top_ref, low_ref, pair_ref, ck_ref, cv_ref, out_ref, held):
        step = pl.program_id(0)

        @pl.when(step == 0)
        def _():
            x = jnp.concatenate([top_ref[...], low_ref[...]], 0)
            held[2 * depth - 1] = pair_heads(dot_rows(x, ck_ref[...]), dot_rows(x, cv_ref[...]))
            for slot in range(2 * depth - 1):
                half = slot % 2
                held[slot] = pair_ref[slot // 2, half * rows : (half + 1) * rows]

        for i in range(block):
            for j in range(capacity):
                out_ref[i, j] = held[table_ref[j * n_view + step * block + i]]

    operands = (*far, paired, ck, cv)
    return pl.pallas_call(
        kernel,
        grid_spec=pltpu.PrefetchScalarGridSpec(
            num_scalar_prefetch=1,
            grid=(steps,),
            in_specs=[whole(a) for a in operands],
            out_specs=pl.BlockSpec((block, capacity, rows, width), lambda i, t: (i, 0, 0, 0)),
            scratch_shapes=[pltpu.VMEM((2 * depth, rows, width), BF16)],
        ),
        out_shape=jax.ShapeDtypeStruct((n_view, capacity, rows, width), BF16),
        name="pack_items",
    )(table, *operands)


def early_kernel(q_ref, kv_ref, hidden_ref, out_w, down_w, result):
    mixes = []
    for at in range(0, q_ref.shape[2], GROUP):
        pairs = kv_ref[:, at : at + GROUP]
        scores = dot_rows(q_ref[0, :, at : at + GROUP], pairs)
        top = jnp.max(scores, axis=1, keepdims=True)
        weights = jnp.exp2((scores - top) * SCALE_LOG2)
        total = jnp.sum(weights, axis=1, keepdims=True)
        mix = dot(weights.astype(BF16), pairs)
        mixes.append(mix[:, HEAD_DIM:] / total)
    mix = jnp.concatenate(mixes, 1).astype(BF16)
    result[0] = (dot(mix, out_w[...]) + dot(hidden_ref[0], down_w[...])).astype(BF16)


def early_terms(q, kv, hidden, out_w, down_w, first, count):
    depth, rows, width = q.shape
    kv = kv.reshape(depth * rows, width)
    ff, cols = hidden.shape[2], out_w.shape[1]
    return pl.pallas_call(
        early_kernel,
        grid=(count,),
        in_specs=[
            pl.BlockSpec((1, rows, width), lambda i: (first + i, 0, 0)),
            whole(kv),
            pl.BlockSpec((1, rows, ff), lambda i: (first + i, 0, 0)),
            whole(out_w),
            whole(down_w),
        ],
        out_specs=pl.BlockSpec((1, rows, cols), lambda i: (i, 0, 0)),
        out_shape=jax.ShapeDtypeStruct((count, rows, cols), BF16),
        compiler_params=params(24),
        name="early_terms",
    )(q, kv, hidden, out_w, down_w)


def add_pair(ahead, behind, terms, at):
    rows = terms.shape[1] // 2

    def kernel(ahead_ref, behind_ref, term_ref, ahead_out, behind_out):
        def add(received, term):
            return (received.astype(F32) + term.astype(F32)).astype(BF16)

        if ahead.shape[0] < rows:
            n = ahead.shape[0]
            ahead_out[:n] = add(ahead_ref[...], term_ref[0, rows : rows + n])
            ahead_out[n:] = term_ref[0, rows + n :]
            behind_out[:n] = term_ref[0, :n]
            behind_out[n:] = add(behind_ref[...], term_ref[0, n:rows])
        else:
            ahead_out[...] = add(ahead_ref[...], term_ref[0, rows:])
            behind_out[...] = add(behind_ref[...], term_ref[0, :rows])

    shape = jax.ShapeDtypeStruct((rows, terms.shape[2]), BF16)
    return pl.pallas_call(
        kernel,
        grid=(1,),
        in_specs=[whole(ahead), whole(behind), pl.BlockSpec((1, *terms.shape[1:]), lambda i: (at, 0, 0))],
        out_specs=[pl.BlockSpec(shape.shape, lambda i: (0, 0))] * 2,
        out_shape=[shape, shape],
        compiler_params=params(12),
        name="add_pair",
    )(ahead, behind, terms)


def cross_attention(items, counts, me, q, received, strips):
    rows, width = received.shape[1:]
    heads = width // GROUP

    def kernel(item_ref, count_ref, me_ref, q_ref, received_ref, out_ref, held, sems):
        def strip_at(place):
            offset = OFFSETS[0]
            for k in range(1, strips):
                offset = jnp.where(place == k, OFFSETS[k], offset)
            return lax.rem(me_ref[0] + offset, strips)

        def copies(place):
            strip = strip_at(place)
            return [
                pltpu.make_async_copy(
                    received_ref.at[item_ref[k * strips + strip]],
                    held.at[place, pl.ds(k * rows, rows)],
                    sems.at[place, k],
                )
                for k in range(SLOTS)
            ]

        @pl.loop(0, strips)
        def _(place):
            for copy in copies(place):
                copy.start()

        @pl.loop(0, strips)
        def _(place):
            for copy in copies(place):
                copy.wait()
            strip = strip_at(place)
            in_use = lax.broadcasted_iota(jnp.int32, (SLOTS * rows, rows), 0) < count_ref[strip] * rows
            queries = q_ref[place // 2, pl.ds(lax.rem(place, 2) * rows, rows), :]
            for head in range(heads):
                at = head * GROUP
                pairs = held[place, :, at : at + GROUP]
                scores = dot_rows(pairs, queries[:, at : at + GROUP])
                scores = jnp.where(in_use, scores, -1e30)
                top = jnp.max(scores, axis=0, keepdims=True)
                weights = jnp.exp2((scores - top) * SCALE_LOG2)
                total = jnp.sum(weights, axis=0, keepdims=True)
                mix = lax.dot_general(
                    pairs, weights.astype(BF16), (((0,), (0,)), ((), ())), preferred_element_type=F32
                )
                out_ref[strip, head * HEAD_DIM : (head + 1) * HEAD_DIM] = (
                    mix[HEAD_DIM:] / total
                ).astype(BF16)

    smem = pl.BlockSpec(memory_space=pltpu.SMEM)
    return pl.pallas_call(
        kernel,
        in_specs=[smem, smem, smem, pl.BlockSpec(memory_space=pltpu.VMEM), pl.BlockSpec(memory_space=pl.ANY)],
        out_specs=pl.BlockSpec(memory_space=pltpu.VMEM),
        out_shape=jax.ShapeDtypeStruct((strips, width // 2, rows), BF16),
        scratch_shapes=[
            pltpu.VMEM((strips, SLOTS * rows, width), BF16),
            pltpu.SemaphoreType.DMA((strips, SLOTS)),
        ],
        compiler_params=params(20),
        name="cross_attention",
    )(items, counts, me, q, received)


def collect(pieces, far):
    strips = len(pieces) + 1
    rows, cols = pieces[0].shape
    blocks = pieces[: strips // 2] + list(far) + pieces[strips // 2 :]

    def kernel(*refs):
        out_ref, at = refs[-1], 0
        for ref in refs[:-1]:
            n = ref.shape[0]
            out_ref[at // rows, at % rows : at % rows + n] = ref[...]
            at += n

    vmem = pl.BlockSpec(memory_space=pltpu.VMEM)
    return pl.pallas_call(
        kernel,
        in_specs=[vmem] * len(blocks),
        out_specs=vmem,
        out_shape=jax.ShapeDtypeStruct((strips, rows, cols), BF16),
        compiler_params=params(12),
        name="collect",
    )(*blocks)


def earlier(token_rows, ahead, behind, terms, at):
    rows, cols = token_rows.shape

    def kernel(token_ref, ahead_ref, behind_ref, own_ref, out_ref):
        early = ahead_ref[...].astype(F32) + behind_ref[...].astype(F32) + own_ref[0].astype(F32)
        out_ref[...] = token_ref[...].astype(F32) + early

    return pl.pallas_call(
        kernel,
        grid=(1,),
        in_specs=[
            whole(token_rows),
            whole(ahead),
            whole(behind),
            pl.BlockSpec((1, rows, cols), lambda i: (at, 0, 0)),
        ],
        out_specs=whole(token_rows),
        out_shape=jax.ShapeDtypeStruct((rows, cols), F32),
        compiler_params=params(12),
        name="earlier",
    )(token_rows, ahead, behind, terms)


def finish(place, mix, mine, other, base):
    strips, width, half = mine.shape
    cols = 256

    def kernel(place_ref, mix_ref, mine_ref, other_ref, base_ref, out_ref, turned):
        me, side = place_ref[0], place_ref[1]
        step = pl.program_id(0)

        @pl.when(step == 0)
        def _():
            for j in range(strips):
                turned[:, j * width : (j + 1) * width] = mix_ref[lax.rem(me + j, strips)].T

        for weights, part in ((mine_ref, side), (other_ref, 1 - side)):
            total = dot(turned[...], weights[...].reshape(strips * width, cols))
            here = pl.ds(pl.multiple_of(part * half + step * cols, 128), cols)
            out_ref[:, here] = (base_ref[:, here] + total).astype(BF16)

    return pl.pallas_call(
        kernel,
        grid_spec=pltpu.PrefetchScalarGridSpec(
            num_scalar_prefetch=1,
            grid=(half // cols,),
            in_specs=[
                whole(mix),
                pl.BlockSpec((strips, width, cols), lambda i, p: (0, 0, i)),
                pl.BlockSpec((strips, width, cols), lambda i, p: (0, 0, i)),
                whole(base),
            ],
            out_specs=whole(base),
            scratch_shapes=[pltpu.VMEM((mix.shape[2], strips * width), BF16)],
        ),
        out_shape=jax.ShapeDtypeStruct(base.shape, BF16),
        compiler_params=params(24),
        name="finish",
    )(place, mix, mine, other, base)


def routing(source_ids, source_count, my_view, my_strip, n_view, n_strip):
    lists = source_ids.transpose(2, 1, 0).reshape(-1, n_view)
    order = lax.broadcasted_iota(jnp.int32, lists.shape, 0)
    keyed = order * n_strip + lists % n_strip
    match = lists // n_strip == my_view
    first = jnp.min(jnp.where(match, keyed, lists.size * n_strip), axis=0)
    last = jnp.max(jnp.where(match, keyed, -1), axis=0)
    strips = jnp.stack([first, jnp.maximum(last, 0)]) % n_strip
    table = slot_of((strips - my_strip + n_strip) % n_strip)
    mine = lax.dynamic_slice_in_dim(lists, my_view, 1, 1) // n_strip
    count = mine.shape[0]
    earlier = lax.broadcasted_iota(jnp.int32, (count, count), 0) < lax.broadcasted_iota(
        jnp.int32, (count, count), 1
    )
    again = jnp.max(jnp.where(jnp.logical_and(mine == mine.T, earlier), 1, 0), axis=0)
    items = mine[:, 0] * 2 + again
    counts = lax.dynamic_slice_in_dim(source_count, my_view, 1, 0)[0]
    return table.reshape(-1), items, counts


def per_device(
    tokens,
    source_ids,
    source_count,
    self_query,
    self_key,
    self_value,
    self_out,
    cross_query,
    cross_key,
    cross_value,
    cross_out,
    mlp_up,
    mlp_down,
):
    n_view = lax.axis_size("view")
    n_strip = lax.axis_size("strip")
    my_view = lax.axis_index("view")
    my_strip = lax.axis_index("strip")
    side = my_view % 2
    capacity = 2
    routes = routing(source_ids, source_count, my_view, my_strip, n_view, n_strip)
    half = cross_out.shape[1] // 2
    my_half = lax.dynamic_slice_in_dim(cross_out, side * half, half, 1)
    place = jnp.stack([my_strip, side]).astype(jnp.int32)

    weights = [self_query.T, self_key.T, self_value.T, cross_query.T, mlp_up, cross_key.T, cross_value.T]

    def both(up, down):
        return shift(up, n_strip, 1), shift(down, n_strip, -1)

    normed = rms_rows(tokens[0])
    half_rows = normed.shape[0] // 2
    ahead, behind, held = normed, normed, None
    ahead, behind = both(ahead, behind)
    early_ahead, routes, my_half, place = lax.optimization_barrier((ahead, routes, my_half, place))
    table, items, counts = routes
    for step in range(2):
        pair = [ahead if step else early_ahead, behind]
        ahead, behind = both(ahead, behind)
        held = project(pair, weights, held, step, True)
    pair = [ahead, behind]
    far = both(ahead[:half_rows], behind[half_rows:])
    paired = cross_pairs([*pair, normed], weights[5], weights[6], held[4])
    outgoing = pack_items(table, far, paired, weights[5], weights[6], n_view, capacity)
    blocks = [*pair, normed, *far]
    received = lax.all_to_all(outgoing, "view", split_axis=0, concat_axis=0, tiled=True)
    received = received.reshape(n_view * capacity, *outgoing.shape[2:])

    my_half, outgoing, blocks = lax.optimization_barrier((my_half, outgoing, blocks))
    ahead, behind, found = my_half, my_half, {0: my_half}
    for step in range(1, 4):
        ahead, behind = both(ahead, behind)
        found[n_strip - step], found[step] = ahead, behind
    part = my_half.shape[0] // 2
    rest = both(ahead[:part], behind[part:])
    my_halves = collect([found[j] for j in range(n_strip) if j != n_strip // 2], rest)
    other_halves = lax.ppermute(my_halves, "view", [(i, i ^ 1) for i in range(n_view)])

    self_q, self_kv, cross_q, hidden = project(blocks, weights, held[:4], 1, False)
    late = early_terms(self_q, self_kv, hidden, self_out, mlp_down, 2, 2)
    soon = early_terms(self_q, self_kv, hidden, self_out, mlp_down, 1, 1)
    last = early_terms(self_q, self_kv, hidden, self_out, mlp_down, 0, 1)
    rows = normed.shape[0]
    ahead, behind = both(*split(late, 1, rows, rows))
    for terms, at in ((late, 0), (soon, 0), (last, 0)):
        ahead, behind = add_pair(ahead, behind, terms, at)
        ahead, behind = both(ahead, behind)

    cross_mix = cross_attention(items, counts, place[:1], cross_q, received, n_strip)
    cross_mix = lax.all_to_all(cross_mix, "strip", split_axis=0, concat_axis=0, tiled=True)
    base = earlier(tokens[0], ahead, behind, late, 1)
    return finish(place, cross_mix, my_halves, other_halves, base)[None]


def solution(mesh):
    in_specs = (
        P("view", "strip", None),
        P(),
        P(),
        P(None, "strip"),
        P(None, "strip"),
        P(None, "strip"),
        P("strip", None),
        P(None, "strip"),
        P(None, "strip"),
        P(None, "strip"),
        P("strip", None),
        P(None, "strip"),
        P("strip", None),
    )
    out_specs = P("view", "strip", None)

    return jax.shard_map(
        per_device, mesh=mesh, in_specs=in_specs, out_specs=out_specs, check_vma=False
    )
```

```python
import math

import jax
import jax.numpy as jnp
from jax import lax
from jax.experimental import pallas as pl
from jax.experimental.pallas import tpu as pltpu
from jax.sharding import PartitionSpec as P


HEAD_DIM = 64
SLOTS = 5
GROUP = 2 * HEAD_DIM
SCALE_LOG2 = math.log2(math.e) / math.sqrt(HEAD_DIM)
BF16 = jnp.bfloat16
F32 = jnp.float32


def rms_rows(values_in):
    widened = values_in.astype(F32)
    scaled = widened * lax.rsqrt(jnp.mean(widened * widened, axis=-1, keepdims=True) + 1e-06)
    return scaled.astype(BF16)


def ring_pairs(size, step):
    return [(i, (i + step) % size) for i in range(size)]


def shift(value, size, step):
    return lax.ppermute(value, "strip", ring_pairs(size, step))


def pair_heads(keys, values):
    pieces = []
    for at in range(0, keys.shape[1], HEAD_DIM):
        pieces += [keys[:, at : at + HEAD_DIM], values[:, at : at + HEAD_DIM]]
    return jnp.concatenate(pieces, 1).astype(BF16)


def pad_heads(queries):
    return pair_heads(queries, jnp.zeros_like(queries))


def params(mebibytes):
    return pltpu.CompilerParams(vmem_limit_bytes=mebibytes << 20)


def split(array, at, first, count):
    half = count // 2

    def kernel(ref, top_ref, low_ref):
        block = ref.at[at] if array.ndim == 3 else ref
        top_ref[...] = block[first : first + half]
        low_ref[...] = block[first + half : first + count]

    vmem = pl.BlockSpec(memory_space=pltpu.VMEM)
    return pl.pallas_call(
        kernel,
        in_specs=[vmem],
        out_specs=[vmem, vmem],
        out_shape=[jax.ShapeDtypeStruct((half, array.shape[-1]), BF16)] * 2,
        compiler_params=params(12),
        name="split",
    )(array)


def dot(a, b):
    return jnp.dot(a, b, preferred_element_type=F32)


def dot_rows(a, b):
    return lax.dot_general(a, b, (((1,), (1,)), ((), ())), preferred_element_type=F32)


OFFSETS = (7, 1, 6, 2, 5, 3, 0, 4)


def whole(array):
    return pl.BlockSpec(array.shape, lambda *_: (0,) * array.ndim)


def project(blocks, sq, sk, sv, cq, up):
    operands = (*blocks, sq, sk, sv, cq, up)
    count = len(blocks)
    total, width = sum(block.shape[0] for block in blocks), blocks[0].shape[1]
    both = 2 * blocks[0].shape[0]
    cols, ff = sq.shape[0], up.shape[1]
    widths = [2 * cols, 2 * cols, 2 * cols, ff]

    def kernel(*refs):
        q_w, k_w, v_w, cross_w, up_w, self_q, self_kv, cross_q, hidden, held = refs[count:]
        step = pl.program_id(0)

        @pl.when(step == 0)
        def _():
            at = 0
            for ref in refs[:count]:
                held[at : at + ref.shape[0]] = ref[...]
                at += ref.shape[0]

        x = held[pl.ds(pl.multiple_of(step * both, both), both)]
        self_kv[0] = pair_heads(dot_rows(x, k_w[...]), dot_rows(x, v_w[...]))
        self_q[0] = pad_heads(dot_rows(x, q_w[...]))
        cross_q[0] = pad_heads(dot_rows(x, cross_w[...]))
        hidden[0] = jax.nn.gelu(dot(x, up_w[...])).astype(BF16)

    return pl.pallas_call(
        kernel,
        grid=(total // both,),
        in_specs=[whole(a) for a in operands],
        out_specs=[pl.BlockSpec((1, both, n), lambda i: (i, 0, 0)) for n in widths],
        out_shape=[jax.ShapeDtypeStruct((total // both, both, n), BF16) for n in widths],
        scratch_shapes=[pltpu.VMEM((total, width), BF16)],
        name="project",
    )(*operands)


def send_group(group, listing, starts, blocks, ck, cv, shape, outgoing):
    n_view, capacity, rows, width = shape
    strips = sum(block.shape[0] for block in blocks) // rows
    operands = (*blocks, ck, cv)
    count = len(blocks)
    extra = () if outgoing is None else (outgoing,)

    def kernel(list_ref, start_ref, *refs):
        ck_ref, cv_ref = refs[count : count + 2]
        out_ref, held, sems = refs[-3:]
        x = jnp.concatenate([ref[...] for ref in refs[:count]], 0)
        held[...] = pair_heads(dot_rows(x, ck_ref[...]), dot_rows(x, cv_ref[...])).reshape(held.shape)

        def copy(i):
            entry = list_ref[i]
            item = entry // 4
            return pltpu.make_async_copy(
                held.at[lax.rem(entry, 4)], out_ref.at[lax.rem(item, n_view), item // n_view], sems.at[i]
            )

        @pl.loop(start_ref[group], start_ref[group + 1])
        def _(i):
            copy(i).start()

        @pl.loop(start_ref[group], start_ref[group + 1])
        def _(i):
            copy(i).wait()

    return pl.pallas_call(
        kernel,
        grid_spec=pltpu.PrefetchScalarGridSpec(
            num_scalar_prefetch=2,
            grid=(1,),
            in_specs=[whole(a) for a in operands] + [pl.BlockSpec(memory_space=pl.ANY)] * len(extra),
            out_specs=pl.BlockSpec(memory_space=pl.ANY),
            scratch_shapes=[
                pltpu.VMEM((strips, rows, width), BF16),
                pltpu.SemaphoreType.DMA((n_view * capacity,)),
            ],
        ),
        out_shape=pltpu.HBM(shape, BF16),
        input_output_aliases={} if outgoing is None else {2 + len(operands): 0},
        compiler_params=params(12),
        name="send_group",
    )(listing, starts, *operands, *extra)


def early_kernel(q_ref, kv_ref, hidden_ref, out_w, down_w, result):
    mixes = []
    for at in range(0, q_ref.shape[2], GROUP):
        pairs = kv_ref[:, at : at + GROUP]
        scores = dot_rows(q_ref[0, :, at : at + GROUP], pairs)
        top = jnp.max(scores, axis=1, keepdims=True)
        weights = jnp.exp2((scores - top) * SCALE_LOG2)
        total = jnp.sum(weights, axis=1, keepdims=True)
        mix = dot(weights.astype(BF16), pairs)
        mixes.append(mix[:, HEAD_DIM:] / total)
    mix = jnp.concatenate(mixes, 1).astype(BF16)
    result[0] = (dot(mix, out_w[...]) + dot(hidden_ref[0], down_w[...])).astype(BF16)


def early_terms(q, kv, hidden, out_w, down_w, first, count):
    depth, rows, width = q.shape
    kv = kv.reshape(depth * rows, width)
    ff, cols = hidden.shape[2], out_w.shape[1]
    return pl.pallas_call(
        early_kernel,
        grid=(count,),
        in_specs=[
            pl.BlockSpec((1, rows, width), lambda i: (first + i, 0, 0)),
            whole(kv),
            pl.BlockSpec((1, rows, ff), lambda i: (first + i, 0, 0)),
            whole(out_w),
            whole(down_w),
        ],
        out_specs=pl.BlockSpec((1, rows, cols), lambda i: (i, 0, 0)),
        out_shape=jax.ShapeDtypeStruct((count, rows, cols), BF16),
        compiler_params=params(24),
        name="early_terms",
    )(q, kv, hidden, out_w, down_w)


def add_pair(ahead, behind, terms, at):
    rows = terms.shape[1] // 2

    def kernel(ahead_ref, behind_ref, term_ref, ahead_out, behind_out):
        def add(received, term):
            return (received.astype(F32) + term.astype(F32)).astype(BF16)

        if ahead.shape[0] < rows:
            n = ahead.shape[0]
            ahead_out[:n] = add(ahead_ref[...], term_ref[0, rows : rows + n])
            ahead_out[n:] = term_ref[0, rows + n :]
            behind_out[:n] = term_ref[0, :n]
            behind_out[n:] = add(behind_ref[...], term_ref[0, n:rows])
        else:
            ahead_out[...] = add(ahead_ref[...], term_ref[0, rows:])
            behind_out[...] = add(behind_ref[...], term_ref[0, :rows])

    shape = jax.ShapeDtypeStruct((rows, terms.shape[2]), BF16)
    return pl.pallas_call(
        kernel,
        grid=(1,),
        in_specs=[whole(ahead), whole(behind), pl.BlockSpec((1, *terms.shape[1:]), lambda i: (at, 0, 0))],
        out_specs=[pl.BlockSpec(shape.shape, lambda i: (0, 0))] * 2,
        out_shape=[shape, shape],
        compiler_params=params(12),
        name="add_pair",
    )(ahead, behind, terms)


def cross_attention(items, counts, me, q, received, strips):
    rows, width = received.shape[1:]
    heads = width // GROUP

    def kernel(item_ref, count_ref, me_ref, q_ref, received_ref, out_ref, held, sems):
        def strip_at(place):
            offset = OFFSETS[0]
            for k in range(1, strips):
                offset = jnp.where(place == k, OFFSETS[k], offset)
            return lax.rem(me_ref[0] + offset, strips)

        def copies(place):
            strip = strip_at(place)
            return [
                pltpu.make_async_copy(
                    received_ref.at[item_ref[k * strips + strip]],
                    held.at[place, pl.ds(k * rows, rows)],
                    sems.at[place, k],
                )
                for k in range(SLOTS)
            ]

        @pl.loop(0, strips)
        def _(place):
            for copy in copies(place):
                copy.start()

        @pl.loop(0, strips)
        def _(place):
            for copy in copies(place):
                copy.wait()
            strip = strip_at(place)
            in_use = lax.broadcasted_iota(jnp.int32, (SLOTS * rows, rows), 0) < count_ref[strip] * rows
            queries = q_ref[place // 2, pl.ds(lax.rem(place, 2) * rows, rows), :]
            for head in range(heads):
                at = head * GROUP
                pairs = held[place, :, at : at + GROUP]
                scores = dot_rows(pairs, queries[:, at : at + GROUP])
                scores = jnp.where(in_use, scores, -1e30)
                top = jnp.max(scores, axis=0, keepdims=True)
                weights = jnp.exp2((scores - top) * SCALE_LOG2)
                total = jnp.sum(weights, axis=0, keepdims=True)
                mix = lax.dot_general(
                    pairs, weights.astype(BF16), (((0,), (0,)), ((), ())), preferred_element_type=F32
                )
                out_ref[strip, head * HEAD_DIM : (head + 1) * HEAD_DIM] = (
                    mix[HEAD_DIM:] / total
                ).astype(BF16)

    smem = pl.BlockSpec(memory_space=pltpu.SMEM)
    return pl.pallas_call(
        kernel,
        in_specs=[smem, smem, smem, pl.BlockSpec(memory_space=pltpu.VMEM), pl.BlockSpec(memory_space=pl.ANY)],
        out_specs=pl.BlockSpec(memory_space=pltpu.VMEM),
        out_shape=jax.ShapeDtypeStruct((strips, width // 2, rows), BF16),
        scratch_shapes=[
            pltpu.VMEM((strips, SLOTS * rows, width), BF16),
            pltpu.SemaphoreType.DMA((strips, SLOTS)),
        ],
        compiler_params=params(20),
        name="cross_attention",
    )(items, counts, me, q, received)


def collect(pieces, far):
    strips = len(pieces) + 1
    rows, cols = pieces[0].shape
    blocks = pieces[: strips // 2] + list(far) + pieces[strips // 2 :]

    def kernel(*refs):
        out_ref, at = refs[-1], 0
        for ref in refs[:-1]:
            n = ref.shape[0]
            out_ref[at // rows, at % rows : at % rows + n] = ref[...]
            at += n

    vmem = pl.BlockSpec(memory_space=pltpu.VMEM)
    return pl.pallas_call(
        kernel,
        in_specs=[vmem] * len(blocks),
        out_specs=vmem,
        out_shape=jax.ShapeDtypeStruct((strips, rows, cols), BF16),
        compiler_params=params(12),
        name="collect",
    )(*blocks)


def earlier(token_rows, ahead, behind, terms, at):
    rows, cols = token_rows.shape

    def kernel(token_ref, ahead_ref, behind_ref, own_ref, out_ref):
        early = ahead_ref[...].astype(F32) + behind_ref[...].astype(F32) + own_ref[0].astype(F32)
        out_ref[...] = token_ref[...].astype(F32) + early

    return pl.pallas_call(
        kernel,
        grid=(1,),
        in_specs=[
            whole(token_rows),
            whole(ahead),
            whole(behind),
            pl.BlockSpec((1, rows, cols), lambda i: (at, 0, 0)),
        ],
        out_specs=whole(token_rows),
        out_shape=jax.ShapeDtypeStruct((rows, cols), F32),
        compiler_params=params(12),
        name="earlier",
    )(token_rows, ahead, behind, terms)


def finish(place, mix, mine, other, base):
    strips, width, half = mine.shape
    cols = 384

    def kernel(place_ref, mix_ref, mine_ref, other_ref, base_ref, out_ref, turned):
        me, side = place_ref[0], place_ref[1]
        step = pl.program_id(0)

        @pl.when(step == 0)
        def _():
            for j in range(strips):
                turned[:, j * width : (j + 1) * width] = mix_ref[lax.rem(me + j, strips)].T

        for weights, part in ((mine_ref, side), (other_ref, 1 - side)):
            total = dot(turned[...], weights[...].reshape(strips * width, cols))
            here = pl.ds(pl.multiple_of(part * half + step * cols, 128), cols)
            out_ref[:, here] = (base_ref[:, here] + total).astype(BF16)

    return pl.pallas_call(
        kernel,
        grid_spec=pltpu.PrefetchScalarGridSpec(
            num_scalar_prefetch=1,
            grid=(half // cols,),
            in_specs=[
                whole(mix),
                pl.BlockSpec((strips, width, cols), lambda i, p: (0, 0, i)),
                pl.BlockSpec((strips, width, cols), lambda i, p: (0, 0, i)),
                whole(base),
            ],
            out_specs=whole(base),
            scratch_shapes=[pltpu.VMEM((mix.shape[2], strips * width), BF16)],
        ),
        out_shape=jax.ShapeDtypeStruct(base.shape, BF16),
        compiler_params=params(24),
        name="finish",
    )(place, mix, mine, other, base)


def by_group(strips, n_strip):
    near = jnp.minimum(strips, n_strip - strips)
    group = jnp.maximum(near - 1, 0)
    behind = jnp.where(strips < n_strip // 2, 1, 0)
    local = jnp.where(near == 0, 2, jnp.where(near == n_strip // 2, 0, behind))
    number = lax.iota(jnp.int32, strips.shape[0])
    entry = number * 4 + local
    rank = group * strips.shape[0] + number
    place = jnp.sum(jnp.where(rank[:, None] < rank[None, :], 1, 0), axis=0)
    listing = jnp.sum(jnp.where(place[:, None] == number[None, :], entry[:, None], 0), axis=0)
    starts = jnp.sum(jnp.where(group[:, None] < lax.iota(jnp.int32, 5)[None, :], 1, 0), axis=0)
    return listing, starts


def routing(source_ids, source_count, my_view, my_strip, n_view, n_strip):
    lists = source_ids.transpose(2, 1, 0).reshape(-1, n_view)
    order = lax.broadcasted_iota(jnp.int32, lists.shape, 0)
    keyed = order * n_strip + lists % n_strip
    match = lists // n_strip == my_view
    first = jnp.min(jnp.where(match, keyed, lists.size * n_strip), axis=0)
    last = jnp.max(jnp.where(match, keyed, -1), axis=0)
    strips = jnp.stack([first, jnp.maximum(last, 0)]) % n_strip
    strips = ((strips - my_strip + n_strip) % n_strip).reshape(-1)
    listing, starts = by_group(strips, n_strip)
    mine = lax.dynamic_slice_in_dim(lists, my_view, 1, 1) // n_strip
    count = mine.shape[0]
    earlier = lax.broadcasted_iota(jnp.int32, (count, count), 0) < lax.broadcasted_iota(
        jnp.int32, (count, count), 1
    )
    again = jnp.max(jnp.where(jnp.logical_and(mine == mine.T, earlier), 1, 0), axis=0)
    items = mine[:, 0] * 2 + again
    counts = lax.dynamic_slice_in_dim(source_count, my_view, 1, 0)[0]
    return listing, starts, items, counts


def per_device(
    tokens,
    source_ids,
    source_count,
    self_query,
    self_key,
    self_value,
    self_out,
    cross_query,
    cross_key,
    cross_value,
    cross_out,
    mlp_up,
    mlp_down,
):
    n_view = lax.axis_size("view")
    n_strip = lax.axis_size("strip")
    my_view = lax.axis_index("view")
    my_strip = lax.axis_index("strip")
    side = my_view % 2
    capacity = 2
    routes = routing(source_ids, source_count, my_view, my_strip, n_view, n_strip)
    half = cross_out.shape[1] // 2
    my_half = lax.dynamic_slice_in_dim(cross_out, side * half, half, 1)
    place = jnp.stack([my_strip, side]).astype(jnp.int32)

    weights = [self_query.T, self_key.T, self_value.T, cross_query.T, mlp_up, cross_key.T, cross_value.T]

    def both(up, down):
        return shift(up, n_strip, 1), shift(down, n_strip, -1)

    normed = rms_rows(tokens[0])
    half_rows = normed.shape[0] // 2
    ahead, behind = both(normed, normed)
    early_ahead, routes, my_half, place = lax.optimization_barrier((ahead, routes, my_half, place))
    listing, starts, items, counts = routes
    shape = (n_view, capacity, normed.shape[0], 2 * cross_key.shape[1])
    outgoing, blocks = None, []
    wanted = [early_ahead, behind, normed]
    for step in range(4):
        blocks += wanted if step else [ahead, behind]
        if step < 2:
            ahead, behind = both(ahead, behind)
        elif step == 2:
            ahead, behind = both(ahead[:half_rows], behind[half_rows:])
        outgoing = send_group(
            step, listing, starts, wanted, weights[5], weights[6], shape, outgoing
        )
        wanted = [ahead, behind]
    blocks = [*blocks[:6], normed, *blocks[6:]]
    received = lax.all_to_all(outgoing, "view", split_axis=0, concat_axis=0, tiled=True)
    received = received.reshape(n_view * capacity, *outgoing.shape[2:])

    my_half, outgoing, blocks = lax.optimization_barrier((my_half, outgoing, blocks))
    ahead, behind, found = my_half, my_half, {0: my_half}
    for step in range(1, 4):
        ahead, behind = both(ahead, behind)
        found[n_strip - step], found[step] = ahead, behind
    part = my_half.shape[0] // 2
    rest = both(ahead[:part], behind[part:])
    my_halves = collect([found[j] for j in range(n_strip) if j != n_strip // 2], rest)
    other_halves = lax.ppermute(my_halves, "view", [(i, i ^ 1) for i in range(n_view)])

    self_q, self_kv, cross_q, hidden = project(blocks, *weights[:5])
    late = early_terms(self_q, self_kv, hidden, self_out, mlp_down, 2, 2)
    soon = early_terms(self_q, self_kv, hidden, self_out, mlp_down, 1, 1)
    last = early_terms(self_q, self_kv, hidden, self_out, mlp_down, 0, 1)
    rows = normed.shape[0]
    ahead, behind = both(*split(late, 1, rows, rows))
    for terms, at in ((late, 0), (soon, 0), (last, 0)):
        ahead, behind = add_pair(ahead, behind, terms, at)
        ahead, behind = both(ahead, behind)

    cross_mix = cross_attention(items, counts, place[:1], cross_q, received, n_strip)
    cross_mix = lax.all_to_all(cross_mix, "strip", split_axis=0, concat_axis=0, tiled=True)
    base = earlier(tokens[0], ahead, behind, late, 1)
    return finish(place, cross_mix, my_halves, other_halves, base)[None]


def solution(mesh):
    in_specs = (
        P("view", "strip", None),
        P(),
        P(),
        P(None, "strip"),
        P(None, "strip"),
        P(None, "strip"),
        P("strip", None),
        P(None, "strip"),
        P(None, "strip"),
        P(None, "strip"),
        P("strip", None),
        P(None, "strip"),
        P("strip", None),
    )
    out_specs = P("view", "strip", None)

    return jax.shard_map(
        per_device, mesh=mesh, in_specs=in_specs, out_specs=out_specs, check_vma=False
    )
```
